32 devices in a mesh: short: 8 (over z, y), long: 4 (over x, core).
Axes of the slice: x: 2, y: 2, z: 4, core: 2. Of those that a mesh axis runs over, the one named last changes fastest.
Arguments:
- query: bfloat16 [32768, 8, 128], P(('long', 'short')), may hold values from -6 to 6
- key: bfloat16 [32768, 8, 128], P(('long', 'short')), may hold values from -6 to 6
- value: bfloat16 [32768, 8, 128], P(('long', 'short')), may hold values from -6 to 6
- level_weight: float32 [8, 20, 32768], P(None, None, ('long', 'short')), may hold values from 0.25 to 1.75
Outputs:
- attended: bfloat16 [32768, 8, 128], P(('long', 'short'))
The draws below stay inside these ranges and needn't reach their ends.
All inputs are finite; a program needn't handle non-finite values.
Results may differ from the reference program's by a relative error of at most 0.0019.
Values sent between devices are 32-bit elements; how exact they have to be, the bound alone decides.
A program may use at most 128 MiB of HBM per device.

```python
import jax
import jax.numpy as jnp
from jax import lax

H = 8
DH = 128
TOK_DEV = 1024
LEVELS = 20
TOKENS = 32768
N_SHORT = 8
N_LONG = 4


def block_scale(stream_key, extent, cuts, smallest, largest):
    def one(axis_at, parts):
        draws = jax.random.uniform(jax.random.fold_in(jax.random.fold_in(stream_key, 6), axis_at), (parts,), jnp.float32, smallest / len(cuts), largest / len(cuts))
        return jnp.repeat(jnp.exp(draws), extent[axis_at] // parts).reshape((-1,) + (1,) * (len(extent) - axis_at - 1))

    level = one(*cuts[0])
    for cut in cuts[1:]:
        level = level * one(*cut)
    return level


def centred(stream_key, dims, deviation, limit, pieces=(), held_as=jnp.bfloat16):
    result = jax.random.normal(stream_key, dims, jnp.float32) * deviation
    if len(pieces) > 0:
        result = block_scale(stream_key, dims, pieces, -0.22, 0.18) * result
    return jnp.clip(result, min=-limit, max=limit).astype(held_as)


def setup_inputs(seed: int = 0) -> dict:
    streams_of = jax.random.split(jax.random.key(seed), 5)
    return {
        "query": centred(streams_of[0], (TOKENS, H, DH), 1.0, 6.0, ((0, 32),)),
        "key": centred(streams_of[1], (TOKENS, H, DH), 1.0, 6.0, ((0, 32),)),
        "value": centred(streams_of[2], (TOKENS, H, DH), 1.0, 6.0, ((0, 32),)),
        "level_weight": jnp.clip(0.25 + 1.5 * jax.random.uniform(streams_of[3], (H, LEVELS, TOKENS), jnp.float32) ** block_scale(streams_of[3], (H, LEVELS, TOKENS), ((2, 32),), -0.2, 0.2), 0.25, 1.75),
    }


EPSILON = 1e-06

def level_table(row_ids, col_ids, local_bits):
    differ = jnp.bitwise_xor(row_ids[:, None], col_ids[None, :])
    levels = jnp.zeros(differ.shape, jnp.int32)
    for bit_no in range(local_bits):
        levels = levels + (differ >= 1 << bit_no).astype(jnp.int32)
    return levels

def near_part(query_blk, key_blk, value_blk, weight_blk):
    length = query_blk.shape[0]
    local_bits = length.bit_length() - 1
    block_rows = min(512, length)
    col_ids = jnp.arange(length, dtype=jnp.int32)
    key_full = key_blk.astype(jnp.float32)
    value_full = value_blk.astype(jnp.float32)
    outputs = []
    for row_start in range(0, length, block_rows):
        row_ids = row_start + jnp.arange(block_rows, dtype=jnp.int32)
        levels = level_table(row_ids, col_ids, local_bits)
        causal = col_ids[None, :] <= row_ids[:, None]
        scores = jnp.einsum('thd,shd->hts', query_blk[row_start:row_start + block_rows].astype(jnp.float32), key_full)
        mixing = jnp.zeros(scores.shape, jnp.float32)
        for level_no in range(local_bits + 1):
            chosen = jnp.where(levels == level_no, 1.0, 0.0).astype(jnp.float32)
            mixing = mixing + chosen[None] * weight_blk[:, level_no, row_start:row_start + block_rows][:, :, None]
        weighted = jnp.where(causal[None], mixing * scores, 0.0).astype(jnp.bfloat16)
        outputs.append(jnp.einsum('hts,she->the', weighted.astype(jnp.float32), value_full))
    return jnp.concatenate(outputs, 0)

def far_part(query_blk, bucket_blk, weight_blk, local_bits):
    bit_count = bucket_blk.shape[0]
    products = jnp.einsum('thd,bhde->bthe', query_blk.astype(jnp.float32), bucket_blk, precision=lax.Precision.HIGHEST)
    gains = jnp.transpose(weight_blk[:, local_bits + 1:local_bits + 1 + bit_count, :], (1, 2, 0))
    return lax.optimization_barrier(jnp.sum(products * gains[..., None], 0))

def finish(total):
    scale = lax.rsqrt(lax.optimization_barrier(jnp.mean(total * total, -1, keepdims=True)) + EPSILON)
    return (total * scale).astype(jnp.bfloat16)

def state_of(inputs):
    return jnp.einsum('thd,the->hde', inputs[0].astype(jnp.float32), inputs[1].astype(jnp.float32))

def reference(query, key, value, level_weight):
    blocks = N_SHORT * N_LONG
    block_bits = blocks.bit_length() - 1
    local_bits = TOK_DEV.bit_length() - 1
    heads = query.shape[1]
    width = query.shape[2]
    query_b = query.reshape(blocks, TOK_DEV, heads, width)
    key_b = key.reshape(blocks, TOK_DEV, heads, width)
    value_b = value.reshape(blocks, TOK_DEV, heads, width)
    weight_b = jnp.transpose(level_weight.reshape(heads, LEVELS, blocks, TOK_DEV), (2, 0, 1, 3))
    states = lax.map(state_of, (key_b, value_b))
    block_ids = jnp.arange(blocks, dtype=jnp.int32)
    level_sum = states
    buckets = []
    for bit_no in range(block_bits):
        partner = jnp.bitwise_xor(block_ids >> bit_no, 1).astype(jnp.int32)
        chosen = jnp.take(level_sum, partner, axis=0)
        is_set = block_ids >> bit_no & 1 == 1
        buckets.append(jnp.where(is_set[:, None, None, None], chosen, 0.0))
        level_sum = level_sum.reshape((-1, 2) + level_sum.shape[1:]).sum(1)
    bucket_all = jnp.stack(buckets, 1)

    def one_block(items):
        query_blk, key_blk, value_blk, weight_blk, bucket_blk = items
        total = near_part(query_blk, key_blk, value_blk, weight_blk) + far_part(query_blk, bucket_blk, weight_blk, local_bits)
        return finish(total)
    attended = lax.map(one_block, (query_b, key_b, value_b, weight_b, bucket_all))
    return attended.reshape(blocks * TOK_DEV, heads, width)
```

```python
import functools

import jax
import jax.numpy as jnp
from jax import lax
from jax.experimental import pallas as pl
from jax.experimental.pallas import tpu as pltpu
from jax.sharding import PartitionSpec as P

EPSILON = 1e-06
TILE = 256
SUB = 128
MESH_ID = pl.DeviceIdType.MESH


def log2(n):
    return n.bit_length() - 1


def flipped(bit, by):
    if isinstance(by, int):
        return 1 - bit if by else bit
    return bit + by - 2 * bit * by


def subsets(bits):
    found = []
    for mask in range(1, 1 << len(bits)):
        found.append(tuple(b for i, b in enumerate(bits) if mask >> i & 1))
    found.sort(key=lambda s: (len(s), [-b for b in reversed(s)]))
    return found


def nt_dot(a, b):
    return lax.dot_general(a, b, (((1,), (1,)), ((), ())), preferred_element_type=jnp.float32)


def kernel(
    short_bits, long_bits, heads, length, width,
    q_ref, k_ref, v_ref, w_ref, out_ref,
    wide_a, wide_b, q_heads, k_heads, v_turned, near, levels, sums, buckets, send_sem, recv_sem,
):
    bits = short_bits + long_bits
    rows = heads * width
    local_bits = log2(length)
    short_pos = lax.axis_index("short")
    long_pos = lax.axis_index("long")
    bit = [(short_pos // (1 << b)) % 2 for b in range(short_bits)]
    bit += [(long_pos // (1 << b)) % 2 for b in range(long_bits)]

    def partner(b):
        if b < short_bits:
            return {"short": short_pos + (1 - 2 * bit[b]) * (1 << b)}
        return {"long": long_pos + (1 - 2 * bit[b]) * (1 << b - short_bits)}

    def split_of(b):
        return list(range(min(b, short_bits))) if b >= 2 else []

    def piece(b, flips):
        split = split_of(b)
        start = 0
        for i, s in enumerate(split):
            start = start + (rows >> i + 1) * flipped(bit[s], 1 if s in flips else 0)
        size = rows >> len(split)
        return pl.ds(pl.multiple_of(start, 8), size)

    number = {}
    for b in range(2):
        number[b] = b * heads
    count = 2 * heads
    for b in range(2, bits):
        for key in [()] + subsets(split_of(b)):
            number[b, key] = count
            count += 1

    def copy(src, dst, where, no, to):
        return pltpu.make_async_remote_copy(
            src_ref=src.at[where], dst_ref=dst.at[where],
            send_sem=send_sem.at[no], recv_sem=recv_sem.at[no],
            device_id=partner(to), device_id_type=MESH_ID,
        )

    barrier = pltpu.get_barrier_semaphore()
    for b in range(bits):
        pl.semaphore_signal(barrier, inc=1, device_id=partner(b), device_id_type=MESH_ID)

    part = 64

    def widen(src, dst):
        def step(i, _):
            at = pl.multiple_of(i * part, part)
            x = src[pl.ds(at, part)].astype(jnp.float32)
            dst[pl.ds(pl.multiple_of(at * heads, part * heads), part * heads), :] = x.reshape(part * heads, width)
            return 0
        lax.fori_loop(0, length // part, step, 0)

    def head_chunk(i, flip0, flip1):
        i0 = i % (heads // 4)
        i1 = (i // (heads // 4)) % 2
        i2 = i // (heads // 2)
        h0 = flipped(bit[0], flipped(i2, flip0))
        h1 = flipped(bit[1], flipped(i1, flip1))
        return h0 * (heads // 2) + h1 * (heads // 4) + i0

    def rows_of(h):
        return pl.ds(pl.multiple_of(h * width, width), width)

    widen(k_ref, wide_a)
    widen(v_ref, wide_b)

    def state_step(i, _):
        h = head_chunk(i, 1, 1)
        key = wide_a[pl.ds(h, length, stride=heads), :].astype(jnp.bfloat16)
        turned = wide_b[pl.ds(h, length, stride=heads), :].T.astype(jnp.bfloat16)
        k_heads[h] = key
        v_turned[h] = turned
        where = rows_of(h)
        sums[0, where, :] = jnp.dot(turned, key, preferred_element_type=jnp.float32)

        @pl.when(i == 0)
        def _():
            pl.semaphore_wait(barrier, bits)

        copy(sums.at[0], buckets.at[0], where, number[0] + i, 0).start()
        return 0

    lax.fori_loop(0, heads, state_step, 0)

    row = lax.broadcasted_iota(jnp.int32, (SUB, SUB), 0)
    col = lax.broadcasted_iota(jnp.int32, (SUB, SUB), 1)
    differ = jnp.bitwise_xor(row, col)
    table = jnp.zeros((SUB, SUB), jnp.int32)
    for b in range(log2(SUB)):
        table = table + (differ >= 1 << b).astype(jnp.int32)
    levels[...] = jnp.where(row <= col, table, -1)

    widen(q_ref, wide_a)

    def near_head(h):
        q_heads[h] = wide_a[pl.ds(h, length, stride=heads), :].astype(jnp.bfloat16)
        level = levels[...]
        for ti in range(length // TILE):
            cols = pl.ds(ti * TILE, TILE)
            query = q_heads[h, cols, :]
            total = None
            for si in range(ti + 1):
                scores = nt_dot(k_heads[h, pl.ds(si * TILE, TILE), :], query)
                if si < ti:
                    weighted = scores * w_ref[h, pl.ds(log2(TILE) + (ti ^ si).bit_length(), 1), cols]
                else:
                    columns = []
                    for a in range(TILE // SUB):
                        at = pl.ds(ti * TILE + a * SUB, SUB)
                        parts = []
                        for c in range(TILE // SUB):
                            block = scores[c * SUB : (c + 1) * SUB, a * SUB : (a + 1) * SUB]
                            if c < a:
                                parts.append(block * w_ref[h, pl.ds(log2(SUB) + (a ^ c).bit_length(), 1), at])
                            elif c > a:
                                parts.append(jnp.zeros_like(block))
                            else:
                                mixing = jnp.zeros((SUB, SUB), jnp.float32)
                                for n in range(log2(SUB) + 1):
                                    mixing = jnp.where(level == n, w_ref[h, pl.ds(n, 1), at], mixing)
                                parts.append(mixing * block)
                        columns.append(jnp.concatenate(parts, 0))
                    weighted = jnp.concatenate(columns, 1)
                product = jnp.dot(
                    v_turned[h, :, pl.ds(si * TILE, TILE)], weighted.astype(jnp.bfloat16),
                    preferred_element_type=jnp.float32,
                )
                total = product if total is None else total + product
            near[h, :, cols] = total

    def received(b, key, where):
        copy(sums.at[b], buckets.at[b], where, number[b, key], b if not key else key[0]).wait_recv()

    def add_up(b, where):
        sums[b + 1, where, :] = sums[b, where, :] + buckets[b, where, :]

    def send_sums(b):
        c = copy(sums.at[b], buckets.at[b], piece(b, ()), number[b, ()], b)
        if b < bits - 1:
            c.start()
        else:
            pl.when(bit[b] == 0)(c.start)

    def pass_on(b, key):
        for g in split_of(b):
            if not key or g < key[0]:
                copy(buckets.at[b], buckets.at[b], piece(b, key), number[b, (g,) + key], g).start()

    def arrive(b):
        if b < bits - 1:
            received(b, (), piece(b, ()))
            add_up(b, piece(b + 1, ()))
            send_sums(b + 1)

            @pl.when(bit[b] == 1)
            def _():
                pass_on(b, ())
        else:
            @pl.when(bit[b] == 1)
            def _():
                received(b, (), piece(b, ()))
                pass_on(b, ())

    def gather(b):
        @pl.when(bit[b] == 1)
        def _():
            for key in subsets(split_of(b)):
                received(b, key, piece(b, key))
                pass_on(b, key)

    def step(i, _):
        near_head(i)
        where = rows_of(head_chunk(i, 0, 1))
        copy(sums.at[0], buckets.at[0], where, number[0] + i, 0).wait_recv()
        add_up(0, where)
        copy(sums.at[1], buckets.at[1], where, number[1] + i, 1).start()

        @pl.when(i == heads // 2)
        def _():
            for n in range(heads // 4):
                own = rows_of(head_chunk(n, 0, 0))
                copy(sums.at[1], buckets.at[1], own, number[1] + n, 1).wait_recv()
            add_up(1, piece(2, ()))
            send_sums(2)

        @pl.when(i == heads - 2)
        def _():
            arrive(2)
        return 0

    lax.fori_loop(0, heads, step, 0)
    for b in range(3, bits):
        arrive(b)

    def rest(n, _):
        own = rows_of(head_chunk(n, 0, 0))
        copy(sums.at[1], buckets.at[1], own, number[1] + n, 1).wait_recv()
        return 0

    lax.fori_loop(heads // 4, heads, rest, 0)
    for b in range(2, bits):
        gather(b)

    def far_head(h, _):
        where = rows_of(h)
        high = []
        low = []
        for b in range(bits):
            full = jnp.where(bit[b] == 1, buckets[b, where, :], 0.0)
            top = full.astype(jnp.bfloat16)
            high.append(top)
            low.append((full - top.astype(jnp.float32)).astype(jnp.bfloat16))
        both = jnp.concatenate([jnp.concatenate(high, 0), jnp.concatenate(low, 0)], 1)
        for ti in range(length // TILE):
            cols = pl.ds(ti * TILE, TILE)
            query = q_heads[h, cols, :]
            products = nt_dot(both, jnp.concatenate([query, query], 1))
            far = None
            for b in range(bits):
                term = products[b * width : (b + 1) * width] * w_ref[h, pl.ds(local_bits + 1 + b, 1), cols]
                far = term if far is None else far + term
            total = near[h, :, cols] + far
            scale = lax.rsqrt(jnp.mean(total * total, 0, keepdims=True) + EPSILON)
            wide_b[pl.ds(ti * TILE * heads + h, TILE, stride=heads), :] = (total * scale).T
        return 0

    lax.fori_loop(0, heads, far_head, 0)

    def narrow(i, _):
        at = pl.multiple_of(i * part, part)
        x = wide_b[pl.ds(pl.multiple_of(at * heads, part * heads), part * heads), :]
        out_ref[pl.ds(at, part)] = x.reshape(part, heads, width).astype(jnp.bfloat16)
        return 0

    lax.fori_loop(0, length // part, narrow, 0)

    def sent(i, _):
        copy(sums.at[0], buckets.at[0], rows_of(head_chunk(i, 1, 1)), number[0] + i, 0).wait_send()
        copy(sums.at[1], buckets.at[1], rows_of(head_chunk(i, 0, 1)), number[1] + i, 1).wait_send()
        return 0

    lax.fori_loop(0, heads, sent, 0)
    for b in range(2, bits):
        c = copy(sums.at[b], buckets.at[b], piece(b, ()), number[b, ()], b)
        if b < bits - 1:
            c.wait_send()
        else:
            pl.when(bit[b] == 0)(c.wait_send)

        @pl.when(bit[b] == 1)
        def _():
            for key in [()] + subsets(split_of(b)):
                for g in split_of(b):
                    if not key or g < key[0]:
                        copy(buckets.at[b], buckets.at[b], piece(b, key), number[b, (g,) + key], g).wait_send()


def per_device(query, key, value, level_weight):
    length, heads, width = query.shape
    short_bits = log2(lax.axis_size("short"))
    long_bits = log2(lax.axis_size("long"))
    bits = short_bits + long_bits
    rows = heads * width
    copies = 2 * heads + sum(1 << min(b, short_bits) for b in range(2, bits))
    vmem = pl.BlockSpec(memory_space=pltpu.VMEM)
    return pl.pallas_call(
        functools.partial(kernel, short_bits, long_bits, heads, length, width),
        out_shape=jax.ShapeDtypeStruct(query.shape, jnp.bfloat16),
        in_specs=[vmem] * 4,
        out_specs=vmem,
        scratch_shapes=[
            pltpu.VMEM((length * heads, width), jnp.float32),
            pltpu.VMEM((length * heads, width), jnp.float32),
            pltpu.VMEM((heads, length, width), jnp.bfloat16),
            pltpu.VMEM((heads, length, width), jnp.bfloat16),
            pltpu.VMEM((heads, width, length), jnp.bfloat16),
            pltpu.VMEM((heads, width, length), jnp.float32),
            pltpu.VMEM((SUB, SUB), jnp.int32),
            pltpu.VMEM((bits, rows, width), jnp.float32),
            pltpu.VMEM((bits, rows, width), jnp.float32),
            pltpu.SemaphoreType.DMA((copies,)),
            pltpu.SemaphoreType.DMA((copies,)),
        ],
        compiler_params=pltpu.CompilerParams(
            collective_id=0, has_side_effects=True, vmem_limit_bytes=60 * 1024 * 1024
        ),
    )(query, key, value, level_weight)


def solution(mesh):
    rows = P(("long", "short"), None, None)
    return jax.shard_map(
        per_device,
        mesh=mesh,
        in_specs=(rows, rows, rows, P(None, None, ("long", "short"))),
        out_specs=rows,
        check_vma=False,
    )
```

```python
import functools

import jax
import jax.numpy as jnp
from jax import lax
from jax.experimental import pallas as pl
from jax.experimental.pallas import tpu as pltpu
from jax.sharding import PartitionSpec as P

EPSILON = 1e-06
TILE = 256
SUB = 128
MESH_ID = pl.DeviceIdType.MESH


def log2(n):
    return n.bit_length() - 1


def flipped(bit, by):
    if isinstance(by, int):
        return 1 - bit if by else bit
    return bit + by - 2 * bit * by


def subsets(bits):
    found = []
    for mask in range(1, 1 << len(bits)):
        found.append(tuple(b for i, b in enumerate(bits) if mask >> i & 1))
    found.sort(key=lambda s: (len(s), [-b for b in reversed(s)]))
    return found


def nt_dot(a, b):
    return lax.dot_general(a, b, (((1,), (1,)), ((), ())), preferred_element_type=jnp.float32)


def kernel(
    short_bits, long_bits, heads, length, width,
    q_ref, k_ref, v_ref, w_ref, out_ref,
    k_in, v_in, q_in, w_in, wide_a, wide_b, q_heads, k_heads, v_turned, near, levels, sums, buckets, send_sem, recv_sem, load_sem,
):
    bits = short_bits + long_bits
    rows = heads * width
    local_bits = log2(length)
    short_pos = lax.axis_index("short")
    long_pos = lax.axis_index("long")
    bit = [(short_pos // (1 << b)) % 2 for b in range(short_bits)]
    bit += [(long_pos // (1 << b)) % 2 for b in range(long_bits)]

    def partner(b):
        if b < short_bits:
            return {"short": short_pos + (1 - 2 * bit[b]) * (1 << b)}
        return {"long": long_pos + (1 - 2 * bit[b]) * (1 << b - short_bits)}

    def split_of(b):
        return list(range(min(b, short_bits))) if b >= 2 else []

    def piece(b, flips):
        split = split_of(b)
        start = 0
        for i, s in enumerate(split):
            start = start + (rows >> i + 1) * flipped(bit[s], 1 if s in flips else 0)
        size = rows >> len(split)
        return pl.ds(pl.multiple_of(start, 8), size)

    number = {}
    for b in range(2):
        number[b] = b * heads
    count = 2 * heads
    for b in range(2, bits):
        for key in [()] + subsets(split_of(b)):
            number[b, key] = count
            count += 1

    def copy(src, dst, where, no, to):
        return pltpu.make_async_remote_copy(
            src_ref=src.at[where], dst_ref=dst.at[where],
            send_sem=send_sem.at[no], recv_sem=recv_sem.at[no],
            device_id=partner(to), device_id_type=MESH_ID,
        )

    barrier = pltpu.get_barrier_semaphore()
    for b in range(bits):
        pl.semaphore_signal(barrier, inc=1, device_id=partner(b), device_id_type=MESH_ID)

    loads = [
        pltpu.make_async_copy(src, dst, load_sem.at[n])
        for n, (src, dst) in enumerate([(k_ref, k_in), (v_ref, v_in), (q_ref, q_in)])
    ]
    for h in range(heads):
        loads.append(pltpu.make_async_copy(w_ref.at[:, h, :], w_in.at[h], load_sem.at[3 + h]))
    for load in loads:
        load.start()

    part = 64

    def widen(src, dst):
        def step(i, _):
            at = pl.multiple_of(i * part, part)
            x = src[pl.ds(at, part)].astype(jnp.float32)
            dst[pl.ds(pl.multiple_of(at * heads, part * heads), part * heads), :] = x.reshape(part * heads, width)
            return 0
        lax.fori_loop(0, length // part, step, 0)

    def head_chunk(i, flip0, flip1):
        i0 = i % (heads // 4)
        i1 = (i // (heads // 4)) % 2
        i2 = i // (heads // 2)
        h0 = flipped(bit[0], flipped(i2, flip0))
        h1 = flipped(bit[1], flipped(i1, flip1))
        return h0 * (heads // 2) + h1 * (heads // 4) + i0

    def rows_of(h):
        return pl.ds(pl.multiple_of(h * width, width), width)

    loads[0].wait()
    widen(k_in, wide_a)
    loads[1].wait()
    widen(v_in, wide_b)

    def state_step(i, _):
        h = head_chunk(i, 1, 1)
        key = wide_a[pl.ds(h, length, stride=heads), :].astype(jnp.bfloat16)
        turned = wide_b[pl.ds(h, length, stride=heads), :].T.astype(jnp.bfloat16)
        k_heads[h] = key
        v_turned[h] = turned
        where = rows_of(h)
        sums[0, where, :] = jnp.dot(turned, key, preferred_element_type=jnp.float32)

        @pl.when(i == 0)
        def _():
            pl.semaphore_wait(barrier, bits)

        copy(sums.at[0], buckets.at[0], where, number[0] + i, 0).start()
        return 0

    lax.fori_loop(0, heads, state_step, 0)

    row = lax.broadcasted_iota(jnp.int32, (SUB, SUB), 0)
    col = lax.broadcasted_iota(jnp.int32, (SUB, SUB), 1)
    differ = jnp.bitwise_xor(row, col)
    table = jnp.zeros((SUB, SUB), jnp.int32)
    for b in range(log2(SUB)):
        table = table + (differ >= 1 << b).astype(jnp.int32)
    levels[...] = jnp.where(row <= col, table, -1)

    loads[2].wait()
    widen(q_in, wide_a)
    for load in loads[3:]:
        load.wait()

    def near_head(h):
        q_heads[h] = wide_a[pl.ds(h, length, stride=heads), :].astype(jnp.bfloat16)
        level = levels[...]
        for ti in range(length // TILE):
            cols = pl.ds(ti * TILE, TILE)
            query = q_heads[h, cols, :]
            total = None
            for si in range(ti + 1):
                scores = nt_dot(k_heads[h, pl.ds(si * TILE, TILE), :], query)
                if si < ti:
                    weighted = scores * w_in[h, pl.ds(log2(TILE) + (ti ^ si).bit_length(), 1), cols]
                else:
                    columns = []
                    for a in range(TILE // SUB):
                        at = pl.ds(ti * TILE + a * SUB, SUB)
                        parts = []
                        for c in range(TILE // SUB):
                            block = scores[c * SUB : (c + 1) * SUB, a * SUB : (a + 1) * SUB]
                            if c < a:
                                parts.append(block * w_in[h, pl.ds(log2(SUB) + (a ^ c).bit_length(), 1), at])
                            elif c > a:
                                parts.append(jnp.zeros_like(block))
                            else:
                                mixing = jnp.zeros((SUB, SUB), jnp.float32)
                                for n in range(log2(SUB) + 1):
                                    mixing = jnp.where(level == n, w_in[h, pl.ds(n, 1), at], mixing)
                                parts.append(mixing * block)
                        columns.append(jnp.concatenate(parts, 0))
                    weighted = jnp.concatenate(columns, 1)
                product = jnp.dot(
                    v_turned[h, :, pl.ds(si * TILE, TILE)], weighted.astype(jnp.bfloat16),
                    preferred_element_type=jnp.float32,
                )
                total = product if total is None else total + product
            near[h, :, cols] = total

    def received(b, key, where):
        copy(sums.at[b], buckets.at[b], where, number[b, key], b if not key else key[0]).wait_recv()

    def add_up(b, where):
        sums[b + 1, where, :] = sums[b, where, :] + buckets[b, where, :]

    def send_sums(b):
        c = copy(sums.at[b], buckets.at[b], piece(b, ()), number[b, ()], b)
        if b < bits - 1:
            c.start()
        else:
            pl.when(bit[b] == 0)(c.start)

    def pass_on(b, key):
        for g in split_of(b):
            if not key or g < key[0]:
                copy(buckets.at[b], buckets.at[b], piece(b, key), number[b, (g,) + key], g).start()

    def arrive(b):
        if b < bits - 1:
            received(b, (), piece(b, ()))
            add_up(b, piece(b + 1, ()))
            send_sums(b + 1)

            @pl.when(bit[b] == 1)
            def _():
                pass_on(b, ())
        else:
            @pl.when(bit[b] == 1)
            def _():
                received(b, (), piece(b, ()))
                pass_on(b, ())

    def gather(b, key):
        @pl.when(bit[b] == 1)
        def _():
            received(b, key, piece(b, key))
            pass_on(b, key)

    def step(i, _):
        where = rows_of(head_chunk(i, 0, 1))
        copy(sums.at[0], buckets.at[0], where, number[0] + i, 0).wait_recv()
        add_up(0, where)
        copy(sums.at[1], buckets.at[1], where, number[1] + i, 1).start()

        @pl.when(i == heads // 2)
        def _():
            for n in range(heads // 4):
                own = rows_of(head_chunk(n, 0, 0))
                copy(sums.at[1], buckets.at[1], own, number[1] + n, 1).wait_recv()
            add_up(1, piece(2, ()))
            send_sums(2)

        near_head(i)
        return 0

    lax.fori_loop(0, heads, step, 0)

    def rest(n, _):
        own = rows_of(head_chunk(n, 0, 0))
        copy(sums.at[1], buckets.at[1], own, number[1] + n, 1).wait_recv()
        return 0

    lax.fori_loop(heads // 4, heads, rest, 0)

    def far_head(h, chosen, last):
        where = rows_of(h)
        high = []
        low = []
        for b in chosen:
            full = jnp.where(bit[b] == 1, buckets[b, where, :], 0.0)
            top = full.astype(jnp.bfloat16)
            high.append(top)
            low.append((full - top.astype(jnp.float32)).astype(jnp.bfloat16))
        both = jnp.concatenate([jnp.concatenate(high, 0), jnp.concatenate(low, 0)], 1)
        for ti in range(length // TILE):
            cols = pl.ds(ti * TILE, TILE)
            query = q_heads[h, cols, :]
            products = nt_dot(both, jnp.concatenate([query, query], 1))
            total = near[h, :, cols]
            for n, b in enumerate(chosen):
                total = total + products[n * width : (n + 1) * width] * w_in[h, pl.ds(local_bits + 1 + b, 1), cols]
            if last:
                scale = lax.rsqrt(jnp.mean(total * total, 0, keepdims=True) + EPSILON)
                wide_b[pl.ds(ti * TILE * heads + h, TILE, stride=heads), :] = (total * scale).T
            else:
                near[h, :, cols] = total

    def far_loop(chosen, last, events):
        def one(h, _):
            for at, work in events:
                pl.when(h == at)(work)
            far_head(h, chosen, last)
            return 0
        lax.fori_loop(0, heads, one, 0)

    far_loop([0, 1], False, [(heads // 2, lambda: arrive(2))])
    waits = [(b, 1 + len(key) + b, key) for b in range(3, bits) for key in [()] + subsets(split_of(b))]
    waits += [(2, 4 + len(key), key) for key in subsets(split_of(2))]
    waits.sort(key=lambda w: (w[1], w[0]))
    early = max(n for n, w in enumerate(waits) if w[0] == 2) + 1

    def work_of(b, key):
        return (lambda: gather(b, key)) if key else (lambda: arrive(b))

    work = [work_of(b, key) for b, _, key in waits]
    for w in work[:early]:
        w()
    late = work[early:]
    far_loop([2], False, [(1 + n * (heads - 1) // len(late), w) for n, w in enumerate(late[: len(late) // 2])])
    for w in late[len(late) // 2 :]:
        w()
    far_loop(list(range(3, bits)), True, [])

    def narrow(i, _):
        at = pl.multiple_of(i * part, part)
        x = wide_b[pl.ds(pl.multiple_of(at * heads, part * heads), part * heads), :]
        out_ref[pl.ds(at, part)] = x.reshape(part, heads, width).astype(jnp.bfloat16)
        return 0

    lax.fori_loop(0, length // part, narrow, 0)

    def sent(i, _):
        copy(sums.at[0], buckets.at[0], rows_of(head_chunk(i, 1, 1)), number[0] + i, 0).wait_send()
        copy(sums.at[1], buckets.at[1], rows_of(head_chunk(i, 0, 1)), number[1] + i, 1).wait_send()
        return 0

    lax.fori_loop(0, heads, sent, 0)
    for b in range(2, bits):
        c = copy(sums.at[b], buckets.at[b], piece(b, ()), number[b, ()], b)
        if b < bits - 1:
            c.wait_send()
        else:
            pl.when(bit[b] == 0)(c.wait_send)

        @pl.when(bit[b] == 1)
        def _():
            for key in [()] + subsets(split_of(b)):
                for g in split_of(b):
                    if not key or g < key[0]:
                        copy(buckets.at[b], buckets.at[b], piece(b, key), number[b, (g,) + key], g).wait_send()


def per_device(query, key, value, level_weight):
    length, heads, width = query.shape
    short_bits = log2(lax.axis_size("short"))
    long_bits = log2(lax.axis_size("long"))
    bits = short_bits + long_bits
    rows = heads * width
    copies = 2 * heads + sum(1 << min(b, short_bits) for b in range(2, bits))
    level_weight = jnp.transpose(level_weight, (1, 0, 2))
    return pl.pallas_call(
        functools.partial(kernel, short_bits, long_bits, heads, length, width),
        out_shape=jax.ShapeDtypeStruct(query.shape, jnp.bfloat16),
        in_specs=[pl.BlockSpec(memory_space=pl.ANY)] * 4,
        out_specs=pl.BlockSpec(memory_space=pltpu.VMEM),
        scratch_shapes=[
            pltpu.VMEM(query.shape, jnp.bfloat16),
            pltpu.VMEM(query.shape, jnp.bfloat16),
            pltpu.VMEM(query.shape, jnp.bfloat16),
            pltpu.VMEM((heads, level_weight.shape[0], length), jnp.float32),
            pltpu.VMEM((length * heads, width), jnp.float32),
            pltpu.VMEM((length * heads, width), jnp.float32),
            pltpu.VMEM((heads, length, width), jnp.bfloat16),
            pltpu.VMEM((heads, length, width), jnp.bfloat16),
            pltpu.VMEM((heads, width, length), jnp.bfloat16),
            pltpu.VMEM((heads, width, length), jnp.float32),
            pltpu.VMEM((SUB, SUB), jnp.int32),
            pltpu.VMEM((bits, rows, width), jnp.float32),
            pltpu.VMEM((bits, rows, width), jnp.float32),
            pltpu.SemaphoreType.DMA((copies,)),
            pltpu.SemaphoreType.DMA((copies,)),
            pltpu.SemaphoreType.DMA((3 + heads,)),
        ],
        compiler_params=pltpu.CompilerParams(
            collective_id=0, has_side_effects=True, vmem_limit_bytes=60 * 1024 * 1024
        ),
    )(query, key, value, level_weight)


def solution(mesh):
    rows = P(("long", "short"), None, None)
    return jax.shard_map(
        per_device,
        mesh=mesh,
        in_specs=(rows, rows, rows, P(None, None, ("long", "short"))),
        out_specs=rows,
        check_vma=False,
    )
```

```python
import functools

import jax
import jax.numpy as jnp
from jax import lax
from jax.experimental import pallas as pl
from jax.experimental.pallas import tpu as pltpu
from jax.sharding import PartitionSpec as P

EPSILON = 1e-06
TILE = 256
SUB = 128
MESH_ID = pl.DeviceIdType.MESH


def log2(n):
    return n.bit_length() - 1


def flipped(bit, by):
    if isinstance(by, int):
        return 1 - bit if by else bit
    return bit + by - 2 * bit * by


def subsets(bits):
    found = [tuple(b for i, b in enumerate(bits) if mask >> i & 1) for mask in range(1 << len(bits))]
    return sorted(found, key=len)


def runs_of(b, short_bits):
    return subsets(list(range(b, short_bits)))


def order_of(b, short_bits):
    if b > short_bits:
        return [short_bits] + list(range(short_bits))
    return list(range(min(b, short_bits)))


def pieces_of(b, short_bits):
    return [(run, key) for run in runs_of(b, short_bits) for key in subsets(order_of(b, short_bits))]


def nt_dot(a, b):
    return lax.dot_general(a, b, (((1,), (1,)), ((), ())), preferred_element_type=jnp.float32)


def kernel(
    short_bits, long_bits, heads, length, width,
    q_ref, k_ref, v_ref, w_ref, out_ref,
    k_in, v_in, q_in, w_in, wide_a, wide_b, q_heads, k_heads, v_turned, near, levels, sums, buckets, send_sem, recv_sem, load_sem,
):
    bits = short_bits + long_bits
    rows = heads * width
    local_bits = log2(length)
    short_pos = lax.axis_index("short")
    long_pos = lax.axis_index("long")
    bit = [(short_pos // (1 << b)) % 2 for b in range(short_bits)]
    bit += [(long_pos // (1 << b)) % 2 for b in range(long_bits)]

    def partner(b):
        if b < short_bits:
            return {"short": short_pos + (1 - 2 * bit[b]) * (1 << b)}
        return {"long": long_pos + (1 - 2 * bit[b]) * (1 << b - short_bits)}

    def piece(b, flips):
        start = 0
        for i in range(short_bits):
            start = start + (rows >> i + 1) * flipped(bit[i], 1 if i in flips else 0)
        size = rows >> short_bits
        if b > short_bits:
            size = size // 2
            start = start + size * flipped(bit[short_bits], 1 if short_bits in flips else 0)
        return pl.ds(pl.multiple_of(start, 8), size)

    number = {}
    for b in range(2):
        number[b] = b * heads
    count = 2 * heads
    for b in range(2, bits):
        for run, key in pieces_of(b, short_bits):
            number[b, run, key] = count
            count += 1

    def copy(src, dst, where, no, to):
        return pltpu.make_async_remote_copy(
            src_ref=src.at[where], dst_ref=dst.at[where],
            send_sem=send_sem.at[no], recv_sem=recv_sem.at[no],
            device_id=partner(to), device_id_type=MESH_ID,
        )

    barrier = pltpu.get_barrier_semaphore()
    for b in range(bits):
        pl.semaphore_signal(barrier, inc=1, device_id=partner(b), device_id_type=MESH_ID)

    loads = [
        pltpu.make_async_copy(src, dst, load_sem.at[n])
        for n, (src, dst) in enumerate([(k_ref, k_in), (v_ref, v_in), (q_ref, q_in)])
    ]
    for h in range(heads):
        loads.append(pltpu.make_async_copy(w_ref.at[:, h, :], w_in.at[h], load_sem.at[3 + h]))
    for load in loads:
        load.start()

    part = 64

    def widen(src, dst):
        def step(i, _):
            at = pl.multiple_of(i * part, part)
            x = src[pl.ds(at, part)].astype(jnp.float32)
            dst[pl.ds(pl.multiple_of(at * heads, part * heads), part * heads), :] = x.reshape(part * heads, width)
            return 0
        lax.fori_loop(0, length // part, step, 0)

    def head_chunk(i, flip0, flip1):
        i0 = i % (heads // 4)
        i1 = (i // (heads // 4)) % 2
        i2 = i // (heads // 2)
        h0 = flipped(bit[0], flipped(i2, flip0))
        h1 = flipped(bit[1], flipped(i1, flip1))
        return h0 * (heads // 2) + h1 * (heads // 4) + i0

    def rows_of(h):
        return pl.ds(pl.multiple_of(h * width, width), width)

    loads[0].wait()
    widen(k_in, wide_a)
    loads[1].wait()
    widen(v_in, wide_b)

    def state_step(i, _):
        h = head_chunk(i, 1, 1)
        key = wide_a[pl.ds(h, length, stride=heads), :].astype(jnp.bfloat16)
        turned = wide_b[pl.ds(h, length, stride=heads), :].T.astype(jnp.bfloat16)
        k_heads[h] = key
        v_turned[h] = turned
        where = rows_of(h)
        sums[0, where, :] = jnp.dot(turned, key, preferred_element_type=jnp.float32)

        @pl.when(i == 0)
        def _():
            pl.semaphore_wait(barrier, bits)

        copy(sums.at[0], buckets.at[0], where, number[0] + i, 0).start()
        return 0

    lax.fori_loop(0, heads, state_step, 0)

    row = lax.broadcasted_iota(jnp.int32, (SUB, SUB), 0)
    col = lax.broadcasted_iota(jnp.int32, (SUB, SUB), 1)
    differ = jnp.bitwise_xor(row, col)
    table = jnp.zeros((SUB, SUB), jnp.int32)
    for b in range(log2(SUB)):
        table = table + (differ >= 1 << b).astype(jnp.int32)
    levels[...] = jnp.where(row <= col, table, -1)

    loads[2].wait()
    widen(q_in, wide_a)
    for load in loads[3:]:
        load.wait()

    def near_head(h):
        q_heads[h] = wide_a[pl.ds(h, length, stride=heads), :].astype(jnp.bfloat16)
        level = levels[...]
        for ti in range(length // TILE):
            cols = pl.ds(ti * TILE, TILE)
            query = q_heads[h, cols, :]
            total = None
            for si in range(ti + 1):
                scores = nt_dot(k_heads[h, pl.ds(si * TILE, TILE), :], query)
                if si < ti:
                    weighted = scores * w_in[h, pl.ds(log2(TILE) + (ti ^ si).bit_length(), 1), cols]
                else:
                    columns = []
                    for a in range(TILE // SUB):
                        at = pl.ds(ti * TILE + a * SUB, SUB)
                        parts = []
                        for c in range(TILE // SUB):
                            block = scores[c * SUB : (c + 1) * SUB, a * SUB : (a + 1) * SUB]
                            if c < a:
                                parts.append(block * w_in[h, pl.ds(log2(SUB) + (a ^ c).bit_length(), 1), at])
                            elif c > a:
                                parts.append(jnp.zeros_like(block))
                            else:
                                mixing = jnp.zeros((SUB, SUB), jnp.float32)
                                for n in range(log2(SUB) + 1):
                                    mixing = jnp.where(level == n, w_in[h, pl.ds(n, 1), at], mixing)
                                parts.append(mixing * block)
                        columns.append(jnp.concatenate(parts, 0))
                    weighted = jnp.concatenate(columns, 1)
                product = jnp.dot(
                    v_turned[h, :, pl.ds(si * TILE, TILE)], weighted.astype(jnp.bfloat16),
                    preferred_element_type=jnp.float32,
                )
                total = product if total is None else total + product
            near[h, :, cols] = total

    def received(b, run, key):
        copy(
            sums.at[b], buckets.at[b], piece(b, run + key), number[b, run, key], key[0] if key else b
        ).wait_recv()

    def add_up(b, where):
        sums[b + 1, where, :] = sums[b, where, :] + buckets[b, where, :]

    def sum_copy(b, run):
        there = tuple(sorted(set(run) ^ {b})) if b < short_bits else run
        return copy(sums.at[b], buckets.at[b], piece(b, run), number[b, there, ()], b)

    def if_needed(b, do):
        if b < bits - 1:
            do()
        else:
            pl.when(bit[b] == 0)(do)

    def shares(b, run, key):
        order = order_of(b, short_bits)
        upto = order.index(key[0]) if key else len(order)
        return [
            copy(buckets.at[b], buckets.at[b], piece(b, run + key), number[b, run, (g,) + key], g)
            for g in reversed(order[:upto])
        ]

    def arrive(b, run):
        if b < bits - 1:
            received(b, run, ())
            if b not in run:
                add_up(b, piece(b, run))
                if_needed(b + 1, lambda: sum_copy(b + 1, run).start())

        @pl.when(bit[b] == 1)
        def _():
            if b == bits - 1:
                received(b, run, ())
            for c in shares(b, run, ()):
                c.start()

    def gather(b, run, key):
        @pl.when(bit[b] == 1)
        def _():
            received(b, run, key)
            for c in shares(b, run, key):
                c.start()

    def time_of(b, run, key):
        base = 2 * (b - 2) + (2 if run else 0)
        return base + 2 * len(key) + 0.1 * b

    events = [(b, run, key) for b in range(2, bits) for run, key in pieces_of(b, short_bits)]
    events.sort(key=lambda e: time_of(*e))
    spot = max(n for n, e in enumerate(events) if e[0] < short_bits) + 1

    def work_of(b, run, key):
        return (lambda: gather(b, run, key)) if key else (lambda: arrive(b, run))

    work = [work_of(*e) for e in events]
    first = 2
    middle = first + (spot - first) * 2 // 3
    late = spot + (len(work) - spot) // 2

    def spread(work, start, stop):
        return [(start + n * (stop - start) // len(work), w) for n, w in enumerate(work)]

    near_events = spread(work[:first], heads - 2, heads)

    def step(i, _):
        where = rows_of(head_chunk(i, 0, 1))
        copy(sums.at[0], buckets.at[0], where, number[0] + i, 0).wait_recv()
        add_up(0, where)
        copy(sums.at[1], buckets.at[1], where, number[1] + i, 1).start()

        @pl.when(i == heads // 4 + 1)
        def _():
            for n in range(heads // 4):
                own = rows_of(head_chunk(n, 0, 0))
                copy(sums.at[1], buckets.at[1], own, number[1] + n, 1).wait_recv()
                add_up(1, own)
            for run in reversed(runs_of(2, short_bits)):
                sum_copy(2, run).start()

        for at, do in near_events:
            pl.when(i == at)(do)
        near_head(i)
        return 0

    lax.fori_loop(0, heads, step, 0)

    def rest(n, _):
        own = rows_of(head_chunk(n, 0, 0))
        copy(sums.at[1], buckets.at[1], own, number[1] + n, 1).wait_recv()
        return 0

    lax.fori_loop(heads // 4, heads, rest, 0)

    def far_head(h, chosen, last):
        where = rows_of(h)
        high = []
        low = []
        for b in chosen:
            full = jnp.where(bit[b] == 1, buckets[b, where, :], 0.0)
            top = full.astype(jnp.bfloat16)
            high.append(top)
            low.append((full - top.astype(jnp.float32)).astype(jnp.bfloat16))
        both = jnp.concatenate([jnp.concatenate(high, 0), jnp.concatenate(low, 0)], 1)
        for ti in range(length // TILE):
            cols = pl.ds(ti * TILE, TILE)
            query = q_heads[h, cols, :]
            products = nt_dot(both, jnp.concatenate([query, query], 1))
            total = near[h, :, cols]
            for n, b in enumerate(chosen):
                total = total + products[n * width : (n + 1) * width] * w_in[h, pl.ds(local_bits + 1 + b, 1), cols]
            if last:
                scale = lax.rsqrt(jnp.mean(total * total, 0, keepdims=True) + EPSILON)
                wide_b[pl.ds(ti * TILE * heads + h, TILE, stride=heads), :] = (total * scale).T
            else:
                near[h, :, cols] = total

    def far_loop(chosen, last, events):
        def one(h, _):
            for at, do in events:
                pl.when(h == at)(do)
            far_head(h, chosen, last)
            return 0
        lax.fori_loop(0, heads, one, 0)

    far_loop([0, 1], False, spread(work[first:middle], 0, heads))
    for do in work[middle:spot]:
        do()
    far_loop(list(range(2, short_bits)), False, spread(work[spot:late], 1, heads))
    for do in work[late:]:
        do()
    far_loop(list(range(short_bits, bits)), True, [])

    def narrow(i, _):
        at = pl.multiple_of(i * part, part)
        x = wide_b[pl.ds(pl.multiple_of(at * heads, part * heads), part * heads), :]
        out_ref[pl.ds(at, part)] = x.reshape(part, heads, width).astype(jnp.bfloat16)
        return 0

    lax.fori_loop(0, length // part, narrow, 0)

    def sent(i, _):
        copy(sums.at[0], buckets.at[0], rows_of(head_chunk(i, 1, 1)), number[0] + i, 0).wait_send()
        copy(sums.at[1], buckets.at[1], rows_of(head_chunk(i, 0, 1)), number[1] + i, 1).wait_send()
        return 0

    lax.fori_loop(0, heads, sent, 0)
    for b in range(2, bits):
        for run in runs_of(b, short_bits):
            if_needed(b, lambda: sum_copy(b, run).wait_send())

        @pl.when(bit[b] == 1)
        def _():
            for run, key in pieces_of(b, short_bits):
                for c in shares(b, run, key):
                    c.wait_send()


def per_device(query, key, value, level_weight):
    length, heads, width = query.shape
    short_bits = log2(lax.axis_size("short"))
    long_bits = log2(lax.axis_size("long"))
    bits = short_bits + long_bits
    rows = heads * width
    copies = 2 * heads + sum(len(pieces_of(b, short_bits)) for b in range(2, bits))
    level_weight = jnp.transpose(level_weight, (1, 0, 2))
    return pl.pallas_call(
        functools.partial(kernel, short_bits, long_bits, heads, length, width),
        out_shape=jax.ShapeDtypeStruct(query.shape, jnp.bfloat16),
        in_specs=[pl.BlockSpec(memory_space=pl.ANY)] * 4,
        out_specs=pl.BlockSpec(memory_space=pltpu.VMEM),
        scratch_shapes=[
            pltpu.VMEM(query.shape, jnp.bfloat16),
            pltpu.VMEM(query.shape, jnp.bfloat16),
            pltpu.VMEM(query.shape, jnp.bfloat16),
            pltpu.VMEM((heads, level_weight.shape[0], length), jnp.float32),
            pltpu.VMEM((length * heads, width), jnp.float32),
            pltpu.VMEM((length * heads, width), jnp.float32),
            pltpu.VMEM((heads, length, width), jnp.bfloat16),
            pltpu.VMEM((heads, length, width), jnp.bfloat16),
            pltpu.VMEM((heads, width, length), jnp.bfloat16),
            pltpu.VMEM((heads, width, length), jnp.float32),
            pltpu.VMEM((SUB, SUB), jnp.int32),
            pltpu.VMEM((bits, rows, width), jnp.float32),
            pltpu.VMEM((bits, rows, width), jnp.float32),
            pltpu.SemaphoreType.DMA((copies,)),
            pltpu.SemaphoreType.DMA((copies,)),
            pltpu.SemaphoreType.DMA((3 + heads,)),
        ],
        compiler_params=pltpu.CompilerParams(
            collective_id=0, has_side_effects=True, vmem_limit_bytes=60 * 1024 * 1024
        ),
    )(query, key, value, level_weight)


def solution(mesh):
    rows = P(("long", "short"), None, None)
    return jax.shard_map(
        per_device,
        mesh=mesh,
        in_specs=(rows, rows, rows, P(None, None, ("long", "short"))),
        out_specs=rows,
        check_vma=False,
    )
```

```python
import functools

import jax
import jax.numpy as jnp
from jax import lax
from jax.experimental import pallas as pl
from jax.experimental.pallas import tpu as pltpu
from jax.sharding import PartitionSpec as P

EPSILON = 1e-06
TILE = 256
SUB = 128
MESH_ID = pl.DeviceIdType.MESH


def log2(n):
    return n.bit_length() - 1


def flipped(bit, by):
    if isinstance(by, int):
        return 1 - bit if by else bit
    return bit + by - 2 * bit * by


def subsets(bits):
    found = [tuple(b for i, b in enumerate(bits) if mask >> i & 1) for mask in range(1 << len(bits))]
    return sorted(found, key=len)


def runs_of(b, short_bits):
    return subsets(list(range(b, short_bits)))


def order_of(b, short_bits):
    if b > short_bits:
        return [short_bits] + list(range(short_bits))
    return list(range(min(b, short_bits)))


def pieces_of(b, short_bits):
    return [(run, key) for run in runs_of(b, short_bits) for key in subsets(order_of(b, short_bits))]


def nt_dot(a, b):
    return lax.dot_general(a, b, (((1,), (1,)), ((), ())), preferred_element_type=jnp.float32)


def kernel(
    short_bits, long_bits, heads, length, width,
    q_ref, k_ref, v_ref, w_ref, out_ref,
    k_in, v_in, q_in, w_in, wide_a, wide_b, q_heads, k_heads, v_turned, near, levels, sums, buckets, send_sem, recv_sem, load_sem,
):
    bits = short_bits + long_bits
    rows = heads * width
    local_bits = log2(length)
    short_pos = lax.axis_index("short")
    long_pos = lax.axis_index("long")
    bit = [(short_pos // (1 << b)) % 2 for b in range(short_bits)]
    bit += [(long_pos // (1 << b)) % 2 for b in range(long_bits)]

    def partner(b):
        if b < short_bits:
            return {"short": short_pos + (1 - 2 * bit[b]) * (1 << b)}
        return {"long": long_pos + (1 - 2 * bit[b]) * (1 << b - short_bits)}

    def piece(b, flips):
        start = 0
        for i in range(short_bits):
            start = start + (rows >> i + 1) * flipped(bit[i], 1 if i in flips else 0)
        size = rows >> short_bits
        if b > short_bits:
            size = size // 2
            start = start + size * flipped(bit[short_bits], 1 if short_bits in flips else 0)
        return pl.ds(pl.multiple_of(start, 8), size)

    number = {}
    for b in range(2):
        number[b] = b * heads
    count = 2 * heads
    for b in range(2, bits):
        for run, key in pieces_of(b, short_bits):
            number[b, run, key] = count
            count += 1

    def copy(src, dst, where, no, to):
        return pltpu.make_async_remote_copy(
            src_ref=src.at[where], dst_ref=dst.at[where],
            send_sem=send_sem.at[no], recv_sem=recv_sem.at[no],
            device_id=partner(to), device_id_type=MESH_ID,
        )

    barrier = pltpu.get_barrier_semaphore()
    for b in range(bits):
        pl.semaphore_signal(barrier, inc=1, device_id=partner(b), device_id_type=MESH_ID)

    loads = [
        pltpu.make_async_copy(src, dst, load_sem.at[n])
        for n, (src, dst) in enumerate([(k_ref, k_in), (v_ref, v_in), (q_ref, q_in)])
    ]
    for h in range(heads):
        loads.append(pltpu.make_async_copy(w_ref.at[:, h, :], w_in.at[h], load_sem.at[3 + h]))
    for load in loads:
        load.start()

    part = 64

    def widen(src, dst):
        def step(i, _):
            at = pl.multiple_of(i * part, part)
            x = src[pl.ds(at, part)].astype(jnp.float32)
            dst[pl.ds(pl.multiple_of(at * heads, part * heads), part * heads), :] = x.reshape(part * heads, width)
            return 0
        lax.fori_loop(0, length // part, step, 0)

    def head_chunk(i, flip0, flip1):
        i0 = i % (heads // 4)
        i1 = (i // (heads // 4)) % 2
        i2 = i // (heads // 2)
        h0 = flipped(bit[0], flipped(i2, flip0))
        h1 = flipped(bit[1], flipped(i1, flip1))
        return h0 * (heads // 2) + h1 * (heads // 4) + i0

    def rows_of(h):
        return pl.ds(pl.multiple_of(h * width, width), width)

    loads[0].wait()
    widen(k_in, wide_a)
    loads[1].wait()
    widen(v_in, wide_b)

    def state_step(i, _):
        h = head_chunk(i, 1, 1)
        key = wide_a[pl.ds(h, length, stride=heads), :].astype(jnp.bfloat16)
        turned = wide_b[pl.ds(h, length, stride=heads), :].T.astype(jnp.bfloat16)
        k_heads[h] = key
        v_turned[h] = turned
        where = rows_of(h)
        sums[0, where, :] = jnp.dot(turned, key, preferred_element_type=jnp.float32)

        @pl.when(i == 0)
        def _():
            pl.semaphore_wait(barrier, bits)

        copy(sums.at[0], buckets.at[0], where, number[0] + i, 0).start()
        return 0

    lax.fori_loop(0, heads, state_step, 0)

    row = lax.broadcasted_iota(jnp.int32, (SUB, SUB), 0)
    col = lax.broadcasted_iota(jnp.int32, (SUB, SUB), 1)
    differ = jnp.bitwise_xor(row, col)
    table = jnp.zeros((SUB, SUB), jnp.int32)
    for b in range(log2(SUB)):
        table = table + (differ >= 1 << b).astype(jnp.int32)
    levels[...] = jnp.where(row <= col, table, -1)

    loads[2].wait()
    widen(q_in, wide_a)
    for load in loads[3:]:
        load.wait()

    def near_head(h):
        q_heads[h] = wide_a[pl.ds(h, length, stride=heads), :].astype(jnp.bfloat16)
        level = levels[...]
        for ti in range(length // TILE):
            cols = pl.ds(ti * TILE, TILE)
            query = q_heads[h, cols, :]
            total = None
            for si in range(ti + 1):
                scores = nt_dot(k_heads[h, pl.ds(si * TILE, TILE), :], query)
                if si < ti:
                    weighted = scores * w_in[h, pl.ds(log2(TILE) + (ti ^ si).bit_length(), 1), cols]
                else:
                    columns = []
                    for a in range(TILE // SUB):
                        at = pl.ds(ti * TILE + a * SUB, SUB)
                        parts = []
                        for c in range(TILE // SUB):
                            block = scores[c * SUB : (c + 1) * SUB, a * SUB : (a + 1) * SUB]
                            if c < a:
                                parts.append(block * w_in[h, pl.ds(log2(SUB) + (a ^ c).bit_length(), 1), at])
                            elif c > a:
                                parts.append(jnp.zeros_like(block))
                            else:
                                mixing = jnp.zeros((SUB, SUB), jnp.float32)
                                for n in range(log2(SUB) + 1):
                                    mixing = jnp.where(level == n, w_in[h, pl.ds(n, 1), at], mixing)
                                parts.append(mixing * block)
                        columns.append(jnp.concatenate(parts, 0))
                    weighted = jnp.concatenate(columns, 1)
                product = jnp.dot(
                    v_turned[h, :, pl.ds(si * TILE, TILE)], weighted.astype(jnp.bfloat16),
                    preferred_element_type=jnp.float32,
                )
                total = product if total is None else total + product
            near[h, :, cols] = total

    def received(b, run, key):
        copy(
            sums.at[b], buckets.at[b], piece(b, run + key), number[b, run, key], key[0] if key else b
        ).wait_recv()

    def add_up(b, where):
        sums[b + 1, where, :] = sums[b, where, :] + buckets[b, where, :]

    def sum_copy(b, run):
        there = tuple(sorted(set(run) ^ {b})) if b < short_bits else run
        return copy(sums.at[b], buckets.at[b], piece(b, run), number[b, there, ()], b)

    def if_needed(b, do):
        if b < bits - 1:
            do()
        else:
            pl.when(bit[b] == 0)(do)

    def shares(b, run, key):
        order = order_of(b, short_bits)
        upto = order.index(key[0]) if key else len(order)
        return [
            copy(buckets.at[b], buckets.at[b], piece(b, run + key), number[b, run, (g,) + key], g)
            for g in reversed(order[:upto])
        ]

    def arrive(b, run):
        if b < bits - 1:
            received(b, run, ())
            if b not in run:
                add_up(b, piece(b, run))
                if_needed(b + 1, lambda: sum_copy(b + 1, run).start())

        @pl.when(bit[b] == 1)
        def _():
            if b == bits - 1:
                received(b, run, ())
            for c in shares(b, run, ()):
                c.start()

    def gather(b, run, key):
        @pl.when(bit[b] == 1)
        def _():
            received(b, run, key)
            for c in shares(b, run, key):
                c.start()

    def time_of(b, run, key):
        base = 2 * (b - 2) + (2 if run else 0)
        return base + 2 * len(key) + 0.1 * b

    events = [(b, run, key) for b in range(2, bits) for run, key in pieces_of(b, short_bits)]
    events.sort(key=lambda e: time_of(*e))
    spot = max(n for n, e in enumerate(events) if e[0] < short_bits) + 1

    def work_of(b, run, key):
        return (lambda: gather(b, run, key)) if key else (lambda: arrive(b, run))

    work = [work_of(*e) for e in events]
    first = 4
    middle = first + (spot - first) * 2 // 3
    late = spot + (len(work) - spot) // 2

    def spread(work, start, stop):
        return [(start + n * (stop - start) // len(work), w) for n, w in enumerate(work)]

    near_events = spread(work[:first], heads - 2, heads)

    def step(i, _):
        where = rows_of(head_chunk(i, 0, 1))
        copy(sums.at[0], buckets.at[0], where, number[0] + i, 0).wait_recv()
        add_up(0, where)
        copy(sums.at[1], buckets.at[1], where, number[1] + i, 1).start()

        @pl.when(i == heads // 4 + 1)
        def _():
            for n in range(heads // 4):
                own = rows_of(head_chunk(n, 0, 0))
                copy(sums.at[1], buckets.at[1], own, number[1] + n, 1).wait_recv()
                add_up(1, own)
            for run in reversed(runs_of(2, short_bits)):
                sum_copy(2, run).start()

        for at, do in near_events:
            pl.when(i == at)(do)
        near_head(i)
        return 0

    lax.fori_loop(0, heads, step, 0)

    def rest(n, _):
        own = rows_of(head_chunk(n, 0, 0))
        copy(sums.at[1], buckets.at[1], own, number[1] + n, 1).wait_recv()
        return 0

    lax.fori_loop(heads // 4, heads, rest, 0)

    def far_head(h, chosen, last):
        where = rows_of(h)
        high = []
        low = []
        for b in chosen:
            full = jnp.where(bit[b] == 1, buckets[b, where, :], 0.0)
            top = full.astype(jnp.bfloat16)
            high.append(top)
            low.append((full - top.astype(jnp.float32)).astype(jnp.bfloat16))
        both = jnp.concatenate([jnp.concatenate(high, 0), jnp.concatenate(low, 0)], 1)
        for ti in range(length // TILE):
            cols = pl.ds(ti * TILE, TILE)
            query = q_heads[h, cols, :]
            products = nt_dot(both, jnp.concatenate([query, query], 1))
            total = near[h, :, cols]
            for n, b in enumerate(chosen):
                total = total + products[n * width : (n + 1) * width] * w_in[h, pl.ds(local_bits + 1 + b, 1), cols]
            if last:
                scale = lax.rsqrt(jnp.mean(total * total, 0, keepdims=True) + EPSILON)
                wide_b[pl.ds(ti * TILE * heads + h, TILE, stride=heads), :] = (total * scale).T
            else:
                near[h, :, cols] = total

    def far_loop(chosen, last, events):
        def one(h, _):
            for at, do in events:
                pl.when(h == at)(do)
            far_head(h, chosen, last)
            return 0
        lax.fori_loop(0, heads, one, 0)

    far_loop([0, 1], False, spread(work[first:middle], 0, heads))
    for do in work[middle:spot]:
        do()
    far_loop(list(range(2, short_bits)), False, spread(work[spot:late], 1, heads))
    for do in work[late:]:
        do()
    far_loop(list(range(short_bits, bits)), True, [])

    def narrow(i, _):
        at = pl.multiple_of(i * part, part)
        x = wide_b[pl.ds(pl.multiple_of(at * heads, part * heads), part * heads), :]
        out_ref[pl.ds(at, part)] = x.reshape(part, heads, width).astype(jnp.bfloat16)
        return 0

    lax.fori_loop(0, length // part, narrow, 0)

    def sent(i, _):
        copy(sums.at[0], buckets.at[0], rows_of(head_chunk(i, 1, 1)), number[0] + i, 0).wait_send()
        copy(sums.at[1], buckets.at[1], rows_of(head_chunk(i, 0, 1)), number[1] + i, 1).wait_send()
        return 0

    lax.fori_loop(0, heads, sent, 0)
    for b in range(2, bits):
        for run in runs_of(b, short_bits):
            if_needed(b, lambda: sum_copy(b, run).wait_send())

        @pl.when(bit[b] == 1)
        def _():
            for run, key in pieces_of(b, short_bits):
                for c in shares(b, run, key):
                    c.wait_send()


def per_device(query, key, value, level_weight):
    length, heads, width = query.shape
    short_bits = log2(lax.axis_size("short"))
    long_bits = log2(lax.axis_size("long"))
    bits = short_bits + long_bits
    rows = heads * width
    copies = 2 * heads + sum(len(pieces_of(b, short_bits)) for b in range(2, bits))
    level_weight = jnp.transpose(level_weight, (1, 0, 2))
    return pl.pallas_call(
        functools.partial(kernel, short_bits, long_bits, heads, length, width),
        out_shape=jax.ShapeDtypeStruct(query.shape, jnp.bfloat16),
        in_specs=[pl.BlockSpec(memory_space=pl.ANY)] * 4,
        out_specs=pl.BlockSpec(memory_space=pltpu.VMEM),
        scratch_shapes=[
            pltpu.VMEM(query.shape, jnp.bfloat16),
            pltpu.VMEM(query.shape, jnp.bfloat16),
            pltpu.VMEM(query.shape, jnp.bfloat16),
            pltpu.VMEM((heads, level_weight.shape[0], length), jnp.float32),
            pltpu.VMEM((length * heads, width), jnp.float32),
            pltpu.VMEM((length * heads, width), jnp.float32),
            pltpu.VMEM((heads, length, width), jnp.bfloat16),
            pltpu.VMEM((heads, length, width), jnp.bfloat16),
            pltpu.VMEM((heads, width, length), jnp.bfloat16),
            pltpu.VMEM((heads, width, length), jnp.float32),
            pltpu.VMEM((SUB, SUB), jnp.int32),
            pltpu.VMEM((bits, rows, width), jnp.float32),
            pltpu.VMEM((bits, rows, width), jnp.float32),
            pltpu.SemaphoreType.DMA((copies,)),
            pltpu.SemaphoreType.DMA((copies,)),
            pltpu.SemaphoreType.DMA((3 + heads,)),
        ],
        compiler_params=pltpu.CompilerParams(
            collective_id=0, has_side_effects=True, vmem_limit_bytes=60 * 1024 * 1024
        ),
    )(query, key, value, level_weight)


def solution(mesh):
    rows = P(("long", "short"), None, None)
    return jax.shard_map(
        per_device,
        mesh=mesh,
        in_specs=(rows, rows, rows, P(None, None, ("long", "short"))),
        out_specs=rows,
        check_vma=False,
    )
```
